32 devices in a mesh: tile: 8 (over y, x, core), grp: 4 (over z).
Axes of the slice: x: 2, y: 2, z: 4, core: 2. Of those that a mesh axis runs over, the one named last changes fastest.
Arguments:
- amplitudes: bfloat16 [2, 64, 4096], P(None, 'tile', 'grp'), may hold values from -6 to 6
- integrals: bfloat16 [8, 16, 256, 256], P('tile', 'grp'), may hold values from -0.1875 to 0.1875
- slot_cd: int32 [8, 16], P('tile'), may hold values from 0 to 3
- slot_ab: int32 [8, 16], P('tile'), may hold values from 0 to 2, as said below
Outputs:
- ladder: bfloat16 [2, 64, 4096], P(None, 'grp', 'tile')
The draws below stay inside these ranges and needn't reach their ends.
Inputs may be any that keep to these rules, and one draw needn't show every extreme that they name: `slot_ab`: 2 marks an empty slot. In every grid column one index of grp has all of its 4 slots live.
All inputs are finite; a program needn't handle non-finite values.
Results may differ from the reference program's by a relative error of at most 0.0085.
Values may be sent and summed in bfloat16 or wider, within the bound.
A program may use at most 64 MiB of HBM per device.

```python
import jax
import jax.numpy as jnp
from jax import lax

TW = 256
NT_DEV = 2
BATCH = 2
PAIRS = 64
NT = 16
CT = 4
N_TILE = 8
N_GRP = 4


def live_table(key):
    groups = N_GRP
    key_busy, key_load, key_offset = jax.random.split(jax.random.fold_in(key, 11), 3)
    busiest = jax.random.randint(key_busy, (N_TILE,), 0, groups)
    loads = jax.random.randint(key_load, (N_TILE, groups), 1, max(groups // 3, 1) + 1)
    device_ids = jnp.arange(groups, dtype=jnp.int32)
    loads = jnp.where(device_ids[None, :] == busiest[:, None], groups, loads)
    offsets = jax.random.randint(key_offset, (N_TILE, groups), 0, groups)
    slot_ids = jnp.arange(groups, dtype=jnp.int32)
    shifted = (slot_ids[None, None, :] - offsets[:, :, None]) % groups
    return (shifted < loads[:, :, None]).reshape(N_TILE, groups * groups)


def draw_slot_ab(key, part):
    live = live_table(key)
    chosen = jax.random.randint(jax.random.fold_in(key, 7), (N_TILE, N_GRP * N_GRP), 0, NT_DEV)
    return jnp.where(live, chosen, NT_DEV).astype(jnp.int32)


def touch_ends(entries, key, least, high):
    longest = entries.shape.index(max(entries.shape))
    spots = []
    for shift in (0, 1):
        where = [jax.random.randint(jax.random.fold_in(key, axis), (), 0, length) for axis, length in enumerate(entries.shape)]
        where[longest] = (where[longest] + shift) % entries.shape[longest]
        spots.append(tuple(where))
    return entries.at[spots[0]].set(least).at[spots[1]].set(high)


def levels(key, dims, shards, smallest, high):
    def one(axis_at, blocks):
        heights = jax.random.uniform(jax.random.fold_in(jax.random.fold_in(key, 6), axis_at), (blocks,), jnp.float32, smallest / len(shards), high / len(shards))
        return jnp.repeat(jnp.exp(heights), dims[axis_at] // blocks).reshape((-1,) + (1,) * (len(dims) - axis_at - 1))

    gain = one(*shards[0])
    for cut in shards[1:]:
        gain = gain * one(*cut)
    return gain


def centred(key, shape, scale, bound, cuts=(), kind=jnp.bfloat16):
    loudness = levels(key, shape, cuts, -0.22, 0.18) if cuts else 1.0
    array = jax.random.normal(key, shape, jnp.float32) * scale * loudness
    return jnp.minimum(jnp.maximum(array, -bound), bound).astype(kind)


def setup_inputs(seed: int = 0) -> dict:
    key_list = jax.random.split(jax.random.key(seed), 5)
    return {
        "amplitudes": centred(key_list[0], (BATCH, PAIRS, NT * TW), 1.0, 6.0, ((1, 8), (2, 4))),
        "integrals": centred(key_list[1], (N_TILE, N_GRP * N_GRP, TW, TW), (TW * N_GRP) ** -0.5, 0.1875, ((0, 8), (1, 4))),
        "slot_cd": touch_ends(jax.random.randint(key_list[2], (N_TILE, N_GRP * N_GRP), 0, CT), jax.random.fold_in(key_list[2], 1), 0, CT - 1).astype(jnp.int32),
        "slot_ab": draw_slot_ab(jax.random.fold_in(key_list[4], 71), 0),
    }


def column_block(amplitudes, column_tiles, cd_list, ab_list):
    owners = jnp.arange(N_GRP * N_GRP, dtype=jnp.int32) % N_GRP
    global_cd = (owners * CT + cd_list).astype(jnp.int32)
    tiled = amplitudes.reshape(BATCH, PAIRS, NT, TW)
    picked = jnp.take(tiled, global_cd, axis=2).astype(jnp.float32)
    products = jnp.einsum("bpsc,scd->bpsd", picked, column_tiles.astype(jnp.float32))
    select = (ab_list[:, None] == jnp.arange(NT_DEV, dtype=jnp.int32)[None, :]).astype(jnp.float32)
    summed = jnp.einsum("bpsd,sa->bpad", products, select)
    return summed.reshape(BATCH, PAIRS, NT_DEV * TW)


def reference(amplitudes, integrals, slot_cd, slot_ab):
    def one_column(operands):
        return column_block(amplitudes, operands[0], operands[1], operands[2])

    columns = lax.map(one_column, (integrals, slot_cd, slot_ab))
    ladder = 0.5 * jnp.transpose(columns, (1, 2, 0, 3)).reshape(BATCH, PAIRS, NT * TW)
    return ladder.astype(jnp.bfloat16)
```

```python
import functools

import jax
import jax.numpy as jnp
from jax import lax
from jax.experimental import pallas as pl
from jax.experimental.pallas import tpu as pltpu
from jax.sharding import PartitionSpec as P

MESH = pl.DeviceIdType.MESH
NT_DEV = 2
BATCH = 2
GATHER_LIMIT = 8 * 2**20
ORDERS = (("z", 1, 2, 0), (2, 1, "z", 0))
HOP = {"z": 2.6, 0: 1.1}


def flip(index, mask):
    bit = 1
    while bit <= mask:
        if mask & bit:
            index = index + bit * (1 - 2 * lax.rem(lax.div(index, jnp.int32(bit)), jnp.int32(2)))
        bit *= 2
    return index


def schedule(groups, tiles):
    bits = tiles.bit_length() - 1
    events, sends = [], {}
    for half in range(BATCH):
        named = ORDERS[half % len(ORDERS)]
        extra = [b for b in range(bits) if b not in named]
        order = [d for d in named if d == "z" or d < bits]
        order = order[:-1] + extra + order[-1:]
        frontier = [((half, 0, 0), -1, 0.0)]
        while frontier:
            node, place, when = frontier.pop(0)
            sends[node] = []
            for at in range(place + 1, len(order)):
                dim = order[at]
                if dim == "z":
                    reached = [(half, dz, node[2]) for dz in range(1, groups)]
                else:
                    reached = [(half, node[1], node[2] | (1 << dim))]
                for child in reached:
                    arrives = when + HOP.get(dim, 2.0)
                    sends[node].append((child, dim))
                    events.append((arrives, child))
                    frontier.append((child, at, arrives))
    events.sort()
    return [child for _, child in events], sends


def kernel(groups, tiles, amp_ref, int_ref, cd_ref, ab_ref, out_ref, buf, tile_buf, acc, send_buf, sums_buf,
           cd_smem, ab_smem, local_sem, send_sem, recv_sem, rs_send, rs_recv):
    g, t = lax.axis_index("grp"), lax.axis_index("tile")
    widths = int_ref.shape[-1]
    rows = out_ref.shape[1]
    bits = tiles.bit_length() - 1

    locals_ = [pltpu.make_async_copy(amp_ref.at[h], buf.at[h, g, t], local_sem.at[h]) for h in range(BATCH)]
    cd_copy = pltpu.make_async_copy(cd_ref, cd_smem, local_sem.at[BATCH])
    ab_copy = pltpu.make_async_copy(ab_ref, ab_smem, local_sem.at[BATCH + 1])
    int_copy = pltpu.make_async_copy(int_ref, tile_buf, local_sem.at[BATCH + 2])
    for copy in (*locals_, cd_copy, ab_copy, int_copy):
        copy.start()

    barrier = pltpu.get_barrier_semaphore()
    for dz in range(1, groups):
        pl.semaphore_signal(barrier, inc=1, device_id=(t, lax.rem(g + dz, groups)), device_id_type=MESH)
    for b in range(bits):
        pl.semaphore_signal(barrier, inc=1, device_id=(flip(t, 1 << b), g), device_id_type=MESH)
    pl.semaphore_wait(barrier, groups - 1 + bits)

    events, sends = schedule(groups, tiles)
    number = {node: i for i, node in enumerate(events)}
    copies = {}

    def forward(node):
        half, k, m = node
        block = buf.at[half, lax.rem(g - k + groups, groups), flip(t, m)]
        for child, dim in sends[node]:
            if dim == "z":
                peer = (t, lax.rem(g + child[1], groups))
            else:
                peer = (flip(t, 1 << dim), g)
            copy = pltpu.make_async_remote_copy(
                src_ref=block, dst_ref=block, send_sem=send_sem.at[number[child]], recv_sem=recv_sem.at[number[child]],
                device_id=peer, device_id_type=MESH)
            copy.start()
            copies[child] = copy

    missing = {}
    for half in range(BATCH):
        for k in range(groups):
            missing[half, k] = tiles
    started = set()
    scatters = []

    def arrived(node):
        half, k, _ = node
        missing[half, k] -= 1
        if missing[half, k]:
            return
        j = lax.rem(g - k + groups, groups)
        cd = cd_smem[0, g * groups + j]
        ab = ab_smem[0, g * groups + j]
        operand = None
        for c in range(buf.shape[-1] // widths):
            chosen = jnp.full((1, 1, widths), (cd == c).astype(jnp.float32)).astype(buf.dtype)
            part = buf[half, j, :, :, c * widths:(c + 1) * widths] * chosen
            operand = part if operand is None else operand + part
        product = jnp.dot(operand.reshape(-1, widths), tile_buf[0, j], preferred_element_type=jnp.float32)
        for a in range(NT_DEV):
            span = slice(a * widths, (a + 1) * widths)
            term = product * (ab == a).astype(jnp.float32)
            if half in started:
                acc[half, :, span] += term
            else:
                acc[half, :, span] = term
        started.add(half)
        if all(missing[half, q] == 0 for q in range(groups)):
            scatter(half)

    def scatter(half):
        for dz in range(1, groups):
            peer = lax.rem(g + dz, groups)
            piece = acc[half, pl.ds(pl.multiple_of(peer * rows, rows), rows), :]
            send_buf[half, dz - 1] = piece.astype(send_buf.dtype)
            slot = half * (groups - 1) + dz - 1
            copy = pltpu.make_async_remote_copy(
                src_ref=send_buf.at[half, dz - 1], dst_ref=sums_buf.at[half, dz - 1], send_sem=rs_send.at[slot],
                recv_sem=rs_recv.at[slot], device_id=(t, peer), device_id_type=MESH)
            copy.start()
            scatters.append((half, copy))

    for half in range(BATCH):
        locals_[half].wait()
        forward((half, 0, 0))
    for copy in (cd_copy, ab_copy, int_copy):
        copy.wait()
    for half in range(BATCH):
        arrived((half, 0, 0))
    for node in events:
        copies[node].wait_recv()
        forward(node)
        arrived(node)

    for half in range(BATCH):
        total = acc[half, pl.ds(pl.multiple_of(g * rows, rows), rows), :]
        mine = [copy for owner, copy in scatters if owner == half]
        for dz, copy in enumerate(mine):
            copy.wait_recv()
            total = total + sums_buf[half, dz].astype(jnp.float32)
        out_ref[half] = (0.5 * total).astype(out_ref.dtype)
    for node in events:
        copies[node].wait_send()
    for _, copy in scatters:
        copy.wait_send()


def fused(groups, tiles, amplitudes, integrals, slot_cd, slot_ab):
    batch, pairs_dev, span = amplitudes.shape
    widths = integrals.shape[-1]
    pairs = pairs_dev * tiles
    rows = pairs // groups
    result = NT_DEV * widths
    events, _ = schedule(groups, tiles)
    count = len(events)
    any_spec = pl.BlockSpec(memory_space=pl.ANY)
    return pl.pallas_call(
        functools.partial(kernel, groups, tiles),
        out_shape=jax.ShapeDtypeStruct((batch, rows, result), jnp.bfloat16),
        in_specs=[any_spec] * 4,
        out_specs=pl.BlockSpec(memory_space=pltpu.VMEM),
        scratch_shapes=[
            pltpu.VMEM((batch, groups, tiles, pairs_dev, span), jnp.bfloat16),
            pltpu.VMEM(integrals.shape, jnp.bfloat16),
            pltpu.VMEM((batch, pairs, result), jnp.float32),
            pltpu.VMEM((batch, groups - 1, rows, result), jnp.bfloat16),
            pltpu.VMEM((batch, groups - 1, rows, result), jnp.bfloat16),
            pltpu.SMEM(slot_cd.shape, jnp.int32),
            pltpu.SMEM(slot_ab.shape, jnp.int32),
            pltpu.SemaphoreType.DMA((batch + 3,)),
            pltpu.SemaphoreType.DMA((count,)),
            pltpu.SemaphoreType.DMA((count,)),
            pltpu.SemaphoreType.DMA((batch * (groups - 1),)),
            pltpu.SemaphoreType.DMA((batch * (groups - 1),)),
        ],
        compiler_params=pltpu.CompilerParams(collective_id=0, has_side_effects=True),
    )(amplitudes, integrals, slot_cd, slot_ab)


def accumulate(slot_operands, slot_tiles, ab_list):
    row_count = slot_operands.shape[0]
    widths = slot_tiles.shape[-1]
    products = jnp.einsum(
        "rsc,scd->rsd", slot_operands, slot_tiles, preferred_element_type=jnp.float32
    )
    select = (ab_list[:, None] == jnp.arange(NT_DEV, dtype=jnp.int32)[None, :]).astype(jnp.float32)
    summed = jnp.einsum("rsd,sa->rad", products, select)
    return summed.reshape(row_count, NT_DEV * widths)


def by_slabs(amplitudes, integrals, slot_cd, slot_ab):
    groups = lax.axis_size("grp")
    own_index = lax.axis_index("grp")
    widths = integrals.shape[-1]
    pairs = amplitudes.shape[1] * lax.axis_size("tile")
    cd_table = slot_cd[0].reshape(groups, groups)
    ab_table = slot_ab[0].reshape(groups, groups)
    own_tiles = integrals[0]
    moved_tiles = lax.all_to_all(own_tiles, "grp", split_axis=0, concat_axis=0, tiled=True)
    cd_list = lax.dynamic_index_in_dim(cd_table, own_index, 1, keepdims=False)
    ab_list = lax.dynamic_index_in_dim(ab_table, own_index, 1, keepdims=False)
    outputs = []
    for batch_index in range(BATCH):
        slab_block = lax.all_gather(amplitudes[batch_index], "tile", axis=0, tiled=True)
        blocks = slab_block.reshape(pairs, slab_block.shape[1] // widths, widths)
        operands = jnp.take(blocks, cd_list, axis=1)
        full_terms = accumulate(operands, moved_tiles, ab_list)
        partial_value = lax.psum_scatter(full_terms, "grp", scatter_dimension=0, tiled=True)
        outputs.append((0.5 * partial_value).astype(jnp.bfloat16))
    return jnp.stack(outputs)


def solution(mesh):
    groups, tiles = mesh.shape["grp"], mesh.shape["tile"]

    def per_device(amplitudes, integrals, slot_cd, slot_ab):
        gathered = amplitudes.size * amplitudes.dtype.itemsize * groups * tiles
        if gathered > GATHER_LIMIT or tiles & (tiles - 1):
            return by_slabs(amplitudes, integrals, slot_cd, slot_ab)
        return fused(groups, tiles, amplitudes, integrals, slot_cd, slot_ab)

    return jax.shard_map(
        per_device,
        mesh=mesh,
        in_specs=(
            P(None, "tile", "grp"),
            P("tile", "grp", None, None),
            P("tile", None),
            P("tile", None),
        ),
        out_specs=P(None, "grp", "tile"),
        check_vma=False,
    )
```

```python
import functools

import jax
import jax.numpy as jnp
from jax import lax
from jax.experimental import pallas as pl
from jax.experimental.pallas import tpu as pltpu
from jax.sharding import PartitionSpec as P

MESH = pl.DeviceIdType.MESH
NT_DEV = 2
BATCH = 2
GATHER_LIMIT = 8 * 2**20
CORES = 2


def kernel(groups, places, amp_ref, int_ref, cd_ref, ab_ref, out_ref, buf, tile_buf, acc, send_buf, sums_buf,
           cd_smem, ab_smem, local_sem, z_send, z_recv, p_send, p_recv, c_send, c_recv, rs_send, rs_recv):
    g, t = lax.axis_index("grp"), lax.axis_index("tile")
    place, core = lax.div(t, jnp.int32(CORES)), lax.rem(t, jnp.int32(CORES))
    widths = int_ref.shape[-1]
    pairs_dev = amp_ref.shape[1]
    share = places // groups
    group = [lax.rem(g + k, groups) for k in range(groups)]
    source = [lax.rem(g - k + groups, groups) for k in range(groups)]
    spot = [lax.rem(place + q, places) for q in range(places)]
    origin = [lax.rem(place - q + places, places) for q in range(places)]
    cores = (core, 1 - core)

    amp_copy = pltpu.make_async_copy(amp_ref, buf.at[g, core, place], local_sem.at[0])
    cd_copy = pltpu.make_async_copy(cd_ref, cd_smem, local_sem.at[1])
    ab_copy = pltpu.make_async_copy(ab_ref, ab_smem, local_sem.at[2])
    int_copy = pltpu.make_async_copy(int_ref, tile_buf, local_sem.at[3])
    for copy in (amp_copy, cd_copy, ab_copy, int_copy):
        copy.start()

    barrier = pltpu.get_barrier_semaphore()
    peers = [(t, group[k]) for k in range(1, groups)]
    peers += [(spot[q] * CORES + core, g) for q in range(1, places)]
    peers += [(place * CORES + 1 - core, g)]
    for peer in peers:
        pl.semaphore_signal(barrier, inc=1, device_id=peer, device_id_type=MESH)
    pl.semaphore_wait(barrier, len(peers))

    def remote(src, dst, send, recv, peer):
        copy = pltpu.make_async_remote_copy(
            src_ref=src, dst_ref=dst, send_sem=send, recv_sem=recv, device_id=peer, device_id_type=MESH)
        copy.start()
        return copy

    def spread(k):
        block = buf.at[source[k], core, place]
        return [
            remote(block, block, p_send.at[k, q - 1], p_recv.at[k, q - 1], (spot[q] * CORES + core, g))
            for q in range(1, places)
        ]

    def multiply(k, part):
        j = source[k]
        cd = cd_smem[0, g * groups + j]
        ab = ab_smem[0, g * groups + j]
        operand = None
        for c in range(buf.shape[-1] // widths):
            chosen = jnp.full((1, 1, 1, widths), (cd == c).astype(jnp.float32)).astype(buf.dtype)
            block = buf[j, cores[part], :, :, :, c * widths:(c + 1) * widths] * chosen
            operand = block if operand is None else operand + block
        product = jnp.dot(operand.reshape(-1, widths), tile_buf[0, j], preferred_element_type=jnp.float32)
        product = product.reshape(*operand.shape[:3], widths)
        for a in range(NT_DEV):
            span = slice(a * widths, (a + 1) * widths)
            term = product * (ab == a).astype(jnp.float32)
            if k:
                acc[part, :, :, :, span] += term
            else:
                acc[part, :, :, :, span] = term

    def scatter(part):
        out = []
        for k in range(1, groups):
            piece = acc[part, pl.ds(group[k] * share, share)]
            send_buf[part, k - 1] = piece.astype(send_buf.dtype)
            out.append(remote(send_buf.at[part, k - 1], sums_buf.at[part, k - 1], rs_send.at[part, k - 1],
                              rs_recv.at[part, k - 1], (t, group[k])))
        return out

    amp_copy.wait()
    own = buf.at[g, core, place]
    along = [remote(own, own, z_send.at[k - 1], z_recv.at[k - 1], (t, group[k])) for k in range(1, groups)]
    spreads = [spread(0)]
    for k in range(1, groups):
        along[k - 1].wait_recv()
        spreads.append(spread(k))
    for copy in (cd_copy, ab_copy, int_copy):
        copy.wait()
    crossings = []
    scatters = []
    for k in range(groups):
        for copy in spreads[k]:
            copy.wait_recv()
        half = buf.at[source[k], core]
        crossings.append(remote(half, half, c_send.at[k], c_recv.at[k], (place * CORES + 1 - core, g)))
        multiply(k, 0)
        if k == groups - 1:
            scatters.append(scatter(0))
        if k:
            crossings[k - 1].wait_recv()
            multiply(k - 1, 1)
    crossings[-1].wait_recv()
    multiply(groups - 1, 1)
    scatters.append(scatter(1))

    for part in range(CORES):
        total = acc[part, pl.ds(g * share, share)]
        for k in range(1, groups):
            scatters[part][k - 1].wait_recv()
            total = total + sums_buf[part, k - 1].astype(jnp.float32)
        total = (0.5 * total).astype(out_ref.dtype)
        for at in range(share):
            first = pl.multiple_of((at * CORES + cores[part]) * pairs_dev, pairs_dev)
            out_ref[:, pl.ds(first, pairs_dev), :] = total[at]
    for copy in (*along, *crossings, *(c for group_ in spreads + scatters for c in group_)):
        copy.wait_send()


def fused(groups, tiles, amplitudes, integrals, slot_cd, slot_ab):
    batch, pairs_dev, span = amplitudes.shape
    widths = integrals.shape[-1]
    places = tiles // CORES
    rows = pairs_dev * tiles // groups
    result = NT_DEV * widths
    any_spec = pl.BlockSpec(memory_space=pl.ANY)
    piece = (CORES, groups - 1, places // groups, batch, pairs_dev, result)
    dma = pltpu.SemaphoreType.DMA
    return pl.pallas_call(
        functools.partial(kernel, groups, places),
        out_shape=jax.ShapeDtypeStruct((batch, rows, result), jnp.bfloat16),
        in_specs=[any_spec] * 4,
        out_specs=pl.BlockSpec(memory_space=pltpu.VMEM),
        scratch_shapes=[
            pltpu.VMEM((groups, CORES, places, batch, pairs_dev, span), jnp.bfloat16),
            pltpu.VMEM(integrals.shape, jnp.bfloat16),
            pltpu.VMEM((CORES, places, batch, pairs_dev, result), jnp.float32),
            pltpu.VMEM(piece, jnp.bfloat16),
            pltpu.VMEM(piece, jnp.bfloat16),
            pltpu.SMEM(slot_cd.shape, jnp.int32),
            pltpu.SMEM(slot_ab.shape, jnp.int32),
            dma((4,)),
            dma((groups - 1,)),
            dma((groups - 1,)),
            dma((groups, places - 1)),
            dma((groups, places - 1)),
            dma((groups,)),
            dma((groups,)),
            dma((CORES, groups - 1)),
            dma((CORES, groups - 1)),
        ],
        compiler_params=pltpu.CompilerParams(collective_id=0, has_side_effects=True),
    )(amplitudes, integrals, slot_cd, slot_ab)


def accumulate(slot_operands, slot_tiles, ab_list):
    row_count = slot_operands.shape[0]
    widths = slot_tiles.shape[-1]
    products = jnp.einsum(
        "rsc,scd->rsd", slot_operands, slot_tiles, preferred_element_type=jnp.float32
    )
    select = (ab_list[:, None] == jnp.arange(NT_DEV, dtype=jnp.int32)[None, :]).astype(jnp.float32)
    summed = jnp.einsum("rsd,sa->rad", products, select)
    return summed.reshape(row_count, NT_DEV * widths)


def by_slabs(amplitudes, integrals, slot_cd, slot_ab):
    groups = lax.axis_size("grp")
    own_index = lax.axis_index("grp")
    widths = integrals.shape[-1]
    pairs = amplitudes.shape[1] * lax.axis_size("tile")
    cd_table = slot_cd[0].reshape(groups, groups)
    ab_table = slot_ab[0].reshape(groups, groups)
    own_tiles = integrals[0]
    moved_tiles = lax.all_to_all(own_tiles, "grp", split_axis=0, concat_axis=0, tiled=True)
    cd_list = lax.dynamic_index_in_dim(cd_table, own_index, 1, keepdims=False)
    ab_list = lax.dynamic_index_in_dim(ab_table, own_index, 1, keepdims=False)
    outputs = []
    for batch_index in range(BATCH):
        slab_block = lax.all_gather(amplitudes[batch_index], "tile", axis=0, tiled=True)
        blocks = slab_block.reshape(pairs, slab_block.shape[1] // widths, widths)
        operands = jnp.take(blocks, cd_list, axis=1)
        full_terms = accumulate(operands, moved_tiles, ab_list)
        partial_value = lax.psum_scatter(full_terms, "grp", scatter_dimension=0, tiled=True)
        outputs.append((0.5 * partial_value).astype(jnp.bfloat16))
    return jnp.stack(outputs)


def solution(mesh):
    groups, tiles = mesh.shape["grp"], mesh.shape["tile"]

    def per_device(amplitudes, integrals, slot_cd, slot_ab):
        gathered = amplitudes.size * amplitudes.dtype.itemsize * groups * tiles
        if gathered > GATHER_LIMIT or tiles % (CORES * groups):
            return by_slabs(amplitudes, integrals, slot_cd, slot_ab)
        return fused(groups, tiles, amplitudes, integrals, slot_cd, slot_ab)

    return jax.shard_map(
        per_device,
        mesh=mesh,
        in_specs=(
            P(None, "tile", "grp"),
            P("tile", "grp", None, None),
            P("tile", None),
            P("tile", None),
        ),
        out_specs=P(None, "grp", "tile"),
        check_vma=False,
    )
```
